32 devices in a mesh: dp: 8 (over z, x), mp: 4 (over y, core).
Axes of the slice: x: 2, y: 2, z: 4, core: 2. Of those that a mesh axis runs over, the one named last changes fastest.
Arguments:
- vision: bfloat16 [2048, 3200], P(('dp', 'mp')), may hold values from -6 to 6
- vision_gain: float32 [3200], replicated, may hold values from 0.1 to 1.9
- image_slot: int32 [8], replicated, may hold values from 0 to 15, as said below
- text_embed: bfloat16 [4096, 8192], P('dp', 'mp'), may hold values from -6 to 6
- w_proj: bfloat16 [3200, 8192], P(None, 'mp'), may hold values from -0.109375 to 0.109375
- llm_gain: float32 [8192], P('mp'), may hold values from 0.1 to 1.9
- w_key: bfloat16 [8192, 1024], P('mp'), may hold values from -0.0625 to 0.0625
- w_value: bfloat16 [8192, 1024], P('mp'), may hold values from -0.0625 to 0.0625
- key_grad: bfloat16 [4096, 1024], P('dp', 'mp'), may hold values from -6 to 6
- value_grad: bfloat16 [4096, 1024], P('dp', 'mp'), may hold values from -6 to 6
Outputs:
- key_out: bfloat16 [4096, 1024], P('dp', 'mp')
- value_out: bfloat16 [4096, 1024], P('dp', 'mp')
- text_grad: bfloat16 [4096, 8192], P('dp', 'mp')
- vision_grad: bfloat16 [2048, 3200], P(('dp', 'mp'))
The draws below stay inside these ranges and needn't reach their ends.
Inputs may be any that keep to these rules, and one draw needn't show every extreme that they name: `image_slot`: the 8 entries are different slots. Image i is encoded on index i of dp; slot j covers positions j * 256 to (j + 1) * 256 - 1, so it lies on index j // 2 of dp. One index of dp receives 2 images, every other one at most one.
All inputs are finite; a program needn't handle non-finite values.
Results may differ from the reference program's by a relative error of at most 0.0058.
Values may be sent and summed in bfloat16 or wider, within the bound.
A program may use at most 128 MiB of HBM per device.

```python
import jax
import jax.numpy as jnp
from jax import lax

DV = 3200
D = 8192
KV = 1024
PATCH = 256
SLOT_DEV = 2
IMAGES = 8
TOKENS = 4096


def draw_image_slot(key, part):
    first_key, second_key, third_key, fourth_key = jax.random.split(key, 4)
    count = IMAGES
    sources = jnp.arange(count, dtype=jnp.int32)
    heavy = jax.random.randint(first_key, (), 0, count).astype(jnp.int32)
    before = (heavy - 1) % count
    across = (heavy + 1 - count // 2) % count
    forced = (sources == before) | (sources == across)
    shuffled = jax.random.permutation(second_key, count).astype(jnp.int32)
    score = jnp.where(forced, count + sources, shuffled)
    order = jnp.argsort(score, stable=True).astype(jnp.int32)
    rank = jnp.zeros((count,), jnp.int32).at[order].set(sources)
    other_dest = (heavy + 2 + jax.random.permutation(third_key, count - 2).astype(jnp.int32)) % count
    later = jnp.clip(rank - (SLOT_DEV - 1), 0, count - 3)
    random_within = jax.random.randint(fourth_key, (count,), 0, SLOT_DEV).astype(jnp.int32)
    to_heavy = rank < SLOT_DEV - 1
    dest_of = jnp.where(to_heavy, heavy, other_dest[later])
    within = jnp.where(to_heavy, rank + 1, random_within)
    dest_of = jnp.where(sources == before, heavy, dest_of)
    within = jnp.where(sources == before, 0, within)
    dest_of = jnp.where(sources == across, (heavy + 1) % count, dest_of)
    slots = dest_of * SLOT_DEV + within
    return slots.astype(jnp.int32)


def block_scale(own_key, dims, shards, smallest, high):
    gain = 1.0
    for position, shards_of in shards:
        draws = jax.random.uniform(jax.random.fold_in(jax.random.fold_in(own_key, 6), position), (shards_of,), jnp.float32, smallest / len(shards), high / len(shards))
        gain = gain * jnp.repeat(jnp.exp(draws), dims[position] // shards_of).reshape((-1,) + (1,) * (len(dims) - 1 - position))
    return gain


def noise(stream_key, dims, spread, most, cuts=(), held_as=jnp.bfloat16):
    drawn = jax.random.normal(stream_key, dims, jnp.float32) * spread
    if len(cuts) > 0:
        drawn = block_scale(stream_key, dims, cuts, -0.22, 0.18) * drawn
    return jnp.clip(drawn, min=-most, max=most).astype(held_as)


def setup_inputs(seed: int = 0) -> dict:
    arg_keys = jax.random.split(jax.random.key(seed), 11)
    vision = noise(arg_keys[0], (IMAGES * PATCH, DV), 1.0, 6.0, ((0, 32),))
    vision_gain = jnp.clip(1.0 + 0.18 * jax.random.normal(arg_keys[1], (DV,), jnp.float32), 0.1, 1.9)
    image_slot = draw_image_slot(jax.random.fold_in(arg_keys[10], 71), 0)
    text_embed = noise(arg_keys[3], (TOKENS, D), 1.0, 6.0, ((0, 8), (1, 4)))
    w_proj = noise(arg_keys[4], (DV, D), DV ** -0.5, 0.109375, ((1, 4),))
    llm_gain = jnp.clip(1.0 + 0.18 * jax.random.normal(arg_keys[5], (D,), jnp.float32), 0.1, 1.9)
    w_key = noise(arg_keys[6], (D, KV), D ** -0.5, 0.0625, ((0, 4),))
    w_value = noise(arg_keys[7], (D, KV), D ** -0.5, 0.0625, ((0, 4),))
    key_grad = noise(arg_keys[8], (TOKENS, KV), 1.0, 6.0, ((0, 8), (1, 4)))
    value_grad = noise(arg_keys[9], (TOKENS, KV), 1.0, 6.0, ((0, 8), (1, 4)))
    return dict(vision=vision, vision_gain=vision_gain, image_slot=image_slot, text_embed=text_embed, w_proj=w_proj, llm_gain=llm_gain, w_key=w_key, w_value=w_value, key_grad=key_grad, value_grad=value_grad)


def reference(vision, vision_gain, image_slot, text_embed, w_proj, llm_gain, w_key, w_value, key_grad, value_grad):
    vision_f = vision.astype(jnp.float32)
    vis_scale = lax.rsqrt(lax.optimization_barrier(jnp.mean(vision_f * vision_f, axis=1, keepdims=True)) + 1e-06)
    vis_normed = (vision_f * vis_scale * vision_gain.astype(jnp.float32)).astype(jnp.bfloat16)
    slot_count = TOKENS // PATCH
    onehot = image_slot[:, None] == jnp.arange(slot_count, dtype=jnp.int32)[None, :]
    filled = jnp.any(onehot, axis=0)
    owner = lax.optimization_barrier(jnp.sum(jnp.where(onehot, jnp.arange(IMAGES, dtype=jnp.int32)[:, None], 0), axis=0)).astype(jnp.int32)
    projected = jnp.dot(vis_normed, w_proj, preferred_element_type=jnp.float32).astype(jnp.bfloat16)
    projected = projected.reshape(IMAGES, PATCH, D)
    placed = projected[owner]
    text_blocks = text_embed.reshape(slot_count, PATCH, D)
    embed = jnp.where(filled[:, None, None], placed, text_blocks).reshape(TOKENS, D)
    embed_f = embed.astype(jnp.float32)
    scale = lax.rsqrt(lax.optimization_barrier(jnp.mean(embed_f * embed_f, axis=1, keepdims=True)) + 1e-05)
    gain_f = llm_gain.astype(jnp.float32)
    llm_normed = (embed_f * scale * gain_f).astype(jnp.bfloat16)
    key_out = jnp.dot(llm_normed, w_key, preferred_element_type=jnp.float32).astype(jnp.bfloat16)
    value_out = jnp.dot(llm_normed, w_value, preferred_element_type=jnp.float32).astype(jnp.bfloat16)
    d_normed = jnp.dot(key_grad, w_key.T, preferred_element_type=jnp.float32)
    d_normed = d_normed + jnp.dot(value_grad, w_value.T, preferred_element_type=jnp.float32)
    grad_g = d_normed * gain_f
    inner = lax.optimization_barrier(jnp.sum(grad_g * embed_f, axis=1, keepdims=True))
    d_embed = scale * grad_g - embed_f * scale * scale * scale * (inner / D)
    d_blocks = d_embed.reshape(slot_count, PATCH, D)
    text_grad = jnp.where(filled[:, None, None], 0.0, d_blocks).reshape(TOKENS, D).astype(jnp.bfloat16)
    image_grad = d_blocks[image_slot].reshape(IMAGES * PATCH, D).astype(jnp.bfloat16)
    d_vis = jnp.dot(image_grad, w_proj.T, preferred_element_type=jnp.float32).astype(jnp.bfloat16)
    grad_h = d_vis.astype(jnp.float32) * vision_gain.astype(jnp.float32)
    vis_inner = lax.optimization_barrier(jnp.mean(grad_h * vision_f, axis=1, keepdims=True))
    vision_grad = vis_scale * grad_h - vision_f * vis_scale * vis_scale * vis_scale * vis_inner
    return (key_out, value_out, text_grad, vision_grad.astype(jnp.bfloat16))
```

```python
import jax
import jax.numpy as jnp
from jax import lax
from jax.sharding import PartitionSpec as P

PATCH = 256
F32 = jnp.float32
BF16 = jnp.bfloat16


def shards(vision, vision_gain, image_slot, text_embed, w_proj, llm_gain, w_key, w_value, key_grad, value_grad):
    mp = lax.axis_size("mp")
    here = lax.axis_index("dp")
    tokens_dev, width = text_embed.shape
    slot_dev = tokens_dev // PATCH
    d_model = width * mp
    kvd = key_grad.shape[1]
    vision_f = vision.astype(F32)
    vis_scale = lax.rsqrt(jnp.mean(vision_f * vision_f, axis=1, keepdims=True) + 1e-06)
    vis_normed = (vision_f * vis_scale * vision_gain).astype(BF16)
    vis_all = lax.all_gather(vis_normed, "mp", axis=0, tiled=True)
    grads = jnp.concatenate([key_grad, value_grad], axis=1)
    every = lax.all_gather(grads, "dp", axis=0, tiled=True)
    my_slot = lax.dynamic_index_in_dim(image_slot, here, keepdims=False)
    mine = lax.dynamic_slice_in_dim(every, my_slot * PATCH, PATCH, axis=0)
    both = jnp.concatenate([grads, mine], axis=0)
    stacked = lax.all_gather(both, "mp", axis=0)
    g_key = jnp.concatenate([stacked[m, :, :kvd] for m in range(mp)], axis=1)
    g_val = jnp.concatenate([stacked[m, :, kvd:] for m in range(mp)], axis=1)
    image_embed = jnp.dot(vis_all, w_proj, preferred_element_type=F32).astype(BF16)

    def forward(e):
        ef = e.astype(F32)
        x = (ef * llm_gain).astype(BF16)
        k = jnp.dot(x, w_key, preferred_element_type=F32)
        v = jnp.dot(x, w_value, preferred_element_type=F32)
        return jnp.sum(ef * ef, axis=1), k, v

    sq_t, k_t, v_t = forward(text_embed)
    sq_i, k_i, v_i = forward(image_embed)
    k_all = jnp.concatenate([k_t, k_i], axis=0)
    v_all = jnp.concatenate([v_t, v_i], axis=0)
    inner = jnp.sum(g_key.astype(F32) * k_all + g_val.astype(F32) * v_all, axis=1)
    sq = lax.psum(jnp.concatenate([sq_t, sq_i]), "mp")
    inner = lax.psum(inner, "mp")
    scale = lax.rsqrt(sq / d_model + 1e-05)[:, None]
    kv = jnp.concatenate(
        [a[:, m * kvd:(m + 1) * kvd].astype(BF16) for m in range(mp) for a in (k_all, v_all)], axis=1
    )
    kv_sum = lax.psum_scatter(kv, "mp", scatter_dimension=1, tiled=True)
    kv_out = (kv_sum.astype(F32) * scale).astype(BF16)
    kv_text, kv_img = kv_out[:tokens_dev], kv_out[tokens_dev:]
    kv_every = lax.all_gather(kv_img, "dp", axis=0)
    blocks = []
    fills = []
    for s in range(slot_dev):
        hit = image_slot == here * slot_dev + s
        filled = jnp.any(hit)
        owner = jnp.argmax(hit)
        got = lax.dynamic_index_in_dim(kv_every, owner, keepdims=False)
        blocks.append(jnp.where(filled, got, kv_text[s * PATCH:(s + 1) * PATCH]))
        fills.append(filled)
    kv_final = jnp.concatenate(blocks, axis=0)
    contract = (((1,), (1,)), ((), ()))
    coef = scale * scale * scale * (inner / d_model)[:, None]

    def backward(gk, gv, e, sc, co):
        d = lax.dot_general(gk, w_key, contract, preferred_element_type=F32)
        d = d + lax.dot_general(gv, w_value, contract, preferred_element_type=F32)
        return sc * (d * llm_gain) - e.astype(F32) * co

    t = tokens_dev
    d_image = backward(g_key[t:], g_val[t:], image_embed, scale[t:], coef[t:]).astype(BF16)
    d_rows = lax.dot_general(d_image, w_proj, contract, preferred_element_type=F32).astype(BF16)
    d_vis = lax.psum_scatter(d_rows, "mp", scatter_dimension=0, tiled=True).astype(F32)
    d_text = backward(g_key[:t], g_val[:t], text_embed, scale[:t], coef[:t])
    full = jnp.repeat(jnp.stack(fills), PATCH)[:, None]
    text_grad = jnp.where(full, 0.0, d_text).astype(BF16)
    grad_h = d_vis * vision_gain
    vis_inner = jnp.mean(grad_h * vision_f, axis=1, keepdims=True)
    vision_grad = vis_scale * grad_h - vision_f * vis_scale * vis_scale * vis_scale * vis_inner
    return kv_final[:, :kvd], kv_final[:, kvd:], text_grad, vision_grad.astype(BF16)


def solution(mesh):
    placed = (
        P(("dp", "mp"), None),
        P(),
        P(),
        P("dp", "mp"),
        P(None, "mp"),
        P("mp"),
        P("mp", None),
        P("mp", None),
        P("dp", "mp"),
        P("dp", "mp"),
    )
    return jax.shard_map(
        shards,
        mesh=mesh,
        in_specs=placed,
        out_specs=(P("dp", "mp"), P("dp", "mp"), P("dp", "mp"), P(("dp", "mp"), None)),
        check_vma=False,
    )
```

```python
import functools

import jax
import jax.numpy as jnp
from jax import lax
from jax.experimental import pallas as pl
from jax.experimental.pallas import tpu as pltpu
from jax.sharding import PartitionSpec as P

PATCH = 256
F32 = jnp.float32
BF16 = jnp.bfloat16
NT = (((1,), (1,)), ((), ()))
DMA = pltpu.SemaphoreType.DMA


def nt(a, b):
    return lax.dot_general(a, b, NT, preferred_element_type=F32)


def remote(src, dst, send_sem, recv_sem, device):
    return pltpu.make_async_remote_copy(
        src_ref=src, dst_ref=dst, send_sem=send_sem, recv_sem=recv_sem,
        device_id=device, device_id_type=pl.DeviceIdType.MESH,
    )


def to_rows(sq, inner):
    lane = lax.broadcasted_iota(jnp.int32, (sq.shape[0], 128), 1)
    wide = jnp.where(lane == 0, sq, jnp.where(lane == 1, inner, 0.0))
    return jnp.transpose(wide)[:8]


def to_columns(rows):
    wide = jnp.transpose(jnp.concatenate([rows] * 16, axis=0))
    return wide[:, 0:1], wide[:, 1:2]


def kernel(
    dp, mp, slot_ref, owner_ref, vision_h, vgain, text_h, wp_h, gain, wk_h, wv_h, kg_h, vg_h, kg4, vg4,
    kvt_out, kvs_out, tg_h, vg_out,
    vis, vis_all, text, wp, wk, wv, xt, gk, gv, gik, giv, emb, xi, dimg, dg,
    t_send, t_own, t_l1, t_s2, t_l2, i_send, i_own, i_l1, i_s2, i_l2,
    d_send, d_own, d_l1, d_s2, d_l2, kvt, kvi,
    st_t, sr_t, st_i, sr_i, sc_t, co_t, sc_i, co_i,
    r1k, r1v, s2k, s2v, r2k, r2v, kvb, r3, s4, r4, tg,
    load_sem, ag_s, ag_r, rs_s, rs_r, st_s, st_r, dv_s, dv_r,
    a1_s, a1_r, a2_s, a2_r, b1_s, b1_r, b2_s, b2_r, tg_sem,
):
    me_d = lax.axis_index("dp")
    me = lax.axis_index("mp")
    ycount = mp // 2
    core = lax.rem(me, 2)
    y = lax.div(me, 2)
    partner = y * 2 + (1 - core)
    tokens, width = text.shape
    slots = tokens // PATCH
    kvd = gk.shape[1] // mp
    rows = vis.shape[0]
    dv = vis.shape[1]
    d_model = width * mp
    rb = r1k.shape[1]

    def ynext(k):
        return lax.rem(y + k, ycount)

    def yprev(k):
        return lax.rem(y + ycount - k, ycount)

    def dnext(k):
        return lax.rem(me_d + k, dp)

    def dprev(k):
        return lax.rem(me_d + dp - k, dp)

    def col(m):
        return pl.ds(pl.multiple_of(m * kvd, kvd), kvd)

    sends = []

    def send(*args):
        copy = remote(*args)
        copy.start()
        sends.append(copy)

    loads = [
        (vision_h, vis), (kg_h, gk.at[:, col(me)]), (vg_h, gv.at[:, col(me)]),
        (text_h, text), (wk_h, wk), (wv_h, wv), (wp_h, wp),
        (kg4.at[:, me_d], r1k.at[pl.ds(me_d * slots, slots)]),
        (vg4.at[:, me_d], r1v.at[pl.ds(me_d * slots, slots)]),
    ]
    loads = [pltpu.make_async_copy(a, b, load_sem.at[n]) for n, (a, b) in enumerate(loads)]
    for copy in loads:
        copy.start()

    barrier = pltpu.get_barrier_semaphore()

    @pl.loop(1, dp)
    def _(k):
        pl.semaphore_signal(barrier, inc=1, device_id=(dnext(k), me), device_id_type=pl.DeviceIdType.MESH)

    for k in range(1, mp):
        pl.semaphore_signal(
            barrier, inc=1, device_id=(me_d, lax.rem(me + k, mp)), device_id_type=pl.DeviceIdType.MESH
        )

    loads[0].wait()
    vf = vis[...].astype(F32)
    vscale = lax.rsqrt(jnp.mean(vf * vf, axis=1, keepdims=True) + 1e-06)
    vis_all[me] = (vf * vscale * vgain[...]).astype(BF16)
    pl.semaphore_wait(barrier, dp - 1 + mp - 1)

    def gather_start(g, block):
        for k in range(1, ycount):
            send(block(me), block(me), ag_s.at[g, 0, k], ag_r.at[g, 0, k], (me_d, ynext(k) * 2 + core))
        send(block(me), block(me), ag_s.at[g, 0, 0], ag_r.at[g, 0, 0], (me_d, partner))

    def arrived(block, send_sem, recv_sem):
        remote(block, block, send_sem, recv_sem, (me_d, partner)).wait_recv()

    def gather_relay(g, block):
        for k in range(1, ycount):
            got = block(yprev(k) * 2 + core)
            arrived(got, ag_s.at[g, 0, k], ag_r.at[g, 0, k])
            send(got, got, ag_s.at[g, 1, k], ag_r.at[g, 1, k], (me_d, partner))

    def gather_finish(g, block):
        arrived(block(partner), ag_s.at[g, 0, 0], ag_r.at[g, 0, 0])
        for k in range(1, ycount):
            arrived(block(yprev(k) * 2 + 1 - core), ag_s.at[g, 1, k], ag_r.at[g, 1, k])

    vis_block = lambda m: vis_all.at[m]
    gk_block = lambda m: gk.at[:, col(m)]
    gv_block = lambda m: gv.at[:, col(m)]
    gik_block = lambda m: gik.at[:, col(m)]
    giv_block = lambda m: giv.at[:, col(m)]

    gather_start(0, vis_block)

    mine = pl.ds(me_d * slots, slots)

    def a1(k, which):
        src, dst = ((kg4, r1k), (vg4, r1v))[which]
        return remote(
            src.at[:, dnext(k)], dst.at[mine], a1_s.at[which, k], a1_r.at[which, k], (dnext(k), me)
        )

    @pl.loop(1, dp)
    def _(k):
        a1(k, 0).start()
        a1(k, 1).start()

    loads[1].wait()
    loads[2].wait()
    gather_start(1, gk_block)
    gather_start(2, gv_block)

    def stage(x, n, psend, own, l1):
        def chunk(m):
            k_part = jnp.dot(x[...], wk[:, col(m)], preferred_element_type=F32)
            v_part = jnp.dot(x[...], wv[:, col(m)], preferred_element_type=F32)
            return k_part, v_part

        for k in range(ycount):
            yk = ynext(k)
            k_part, v_part = chunk(yk * 2 + 1 - core)
            psend[yk, :, :kvd] = k_part.astype(BF16)
            psend[yk, :, kvd:] = v_part.astype(BF16)
            send(psend.at[yk], l1.at[yk], rs_s.at[n, 0, k], rs_r.at[n, 0, k], (me_d, partner))
        for k in range(ycount):
            yk = ynext(k)
            k_part, v_part = chunk(yk * 2 + core)
            own[yk, :, :kvd] = k_part
            own[yk, :, kvd:] = v_part

    def level_two(n, own, l1, s2, l2):
        for k in range(ycount - 1, 0, -1):
            yk = ynext(k)
            arrived(l1.at[yk], rs_s.at[n, 0, k], rs_r.at[n, 0, k])
            s2[k] = (own[yk] + l1[yk].astype(F32)).astype(BF16)
            send(s2.at[k], l2.at[k], rs_s.at[n, 1, k], rs_r.at[n, 1, k], (me_d, yk * 2 + core))

    def level_end(n, own, l1, l2):
        arrived(l1.at[y], rs_s.at[n, 0, 0], rs_r.at[n, 0, 0])
        total = own[y] + l1[y].astype(F32)
        for k in range(1, ycount):
            arrived(l2.at[k], rs_s.at[n, 1, k], rs_r.at[n, 1, k])
            total = total + l2[k].astype(F32)
        return total

    def stats_send(n, st, sr):
        for k in range(1, mp):
            send(st, sr.at[k], st_s.at[n, k], st_r.at[n, k], (me_d, lax.rem(me + k, mp)))

    def stats_end(n, st, sr, sc, co):
        total = st[...]
        for k in range(1, mp):
            arrived(sr.at[k], st_s.at[n, k], st_r.at[n, k])
            total = total + sr[k]
        sq, inner = to_columns(total)
        scale = lax.rsqrt(sq / d_model + 1e-05)
        sc[...] = jnp.broadcast_to(scale, sc.shape)
        co[...] = jnp.broadcast_to(scale * scale * scale * (inner / d_model), co.shape)

    loads[3].wait()
    tf = text[...].astype(F32)
    sq_t = jnp.sum(tf * tf, axis=1, keepdims=True)
    xt[...] = (tf * gain[...]).astype(BF16)
    loads[4].wait()
    loads[5].wait()
    stage(xt, 0, t_send, t_own, t_l1)
    gather_relay(0, vis_block)
    level_two(0, t_own, t_l1, t_s2, t_l2)

    loads[7].wait()
    loads[8].wait()

    @pl.loop(1, dp)
    def _(k):
        for which, dst in ((0, r1k), (1, r1v)):
            block = dst.at[pl.ds(dprev(k) * slots, slots)]
            remote(block, block, a1_s.at[which, k], a1_r.at[which, k], (me_d, partner)).wait_recv()

    @pl.loop(0, dp)
    def _(i):
        s2k[i] = r1k[slot_ref[i]]
        s2v[i] = r1v[slot_ref[i]]

    r2k[me_d] = s2k[me_d]
    r2v[me_d] = s2v[me_d]

    def a2(k, which):
        src, dst = ((s2k, r2k), (s2v, r2v))[which]
        return remote(
            src.at[dnext(k)], dst.at[me_d], a2_s.at[which, k], a2_r.at[which, k], (dnext(k), me)
        )

    @pl.loop(1, dp)
    def _(k):
        a2(k, 0).start()
        a2(k, 1).start()

    gather_finish(0, vis_block)
    loads[6].wait()
    step = 256
    dimg_rows = mp * rows


    def project(j, acc):
        cs = pl.ds(pl.multiple_of(j * step, step), step)
        e = jnp.concatenate([vis_all[m] for m in range(mp)], axis=0)
        e = jnp.dot(e, wp[:, cs], preferred_element_type=F32).astype(BF16)
        emb[:, cs] = e
        ef = e.astype(F32)
        xi[:, cs] = (ef * gain[:, cs]).astype(BF16)
        return acc + jnp.sum(ef * ef, axis=1, keepdims=True)

    sq_i = lax.fori_loop(0, width // step, project, jnp.zeros((dimg_rows, 1), F32))
    stage(xi, 1, i_send, i_own, i_l1)
    gather_relay(1, gk_block)
    gather_relay(2, gv_block)
    level_two(1, i_own, i_l1, i_s2, i_l2)

    @pl.loop(1, dp)
    def _(k):
        for which, dst in ((0, r2k), (1, r2v)):
            block = dst.at[dprev(k)]
            remote(block, block, a2_s.at[which, k], a2_r.at[which, k], (me_d, partner)).wait_recv()

    own_k = r2k[...].astype(F32).reshape(PATCH, kvd)
    own_v = r2v[...].astype(F32).reshape(PATCH, kvd)
    gik[:, col(me)] = own_k.astype(BF16)
    giv[:, col(me)] = own_v.astype(BF16)
    gather_start(3, gik_block)
    gather_start(4, giv_block)

    total = level_end(0, t_own, t_l1, t_l2)
    kvt[...] = total
    inner = jnp.sum(
        total[:, :kvd] * gk[:, col(me)].astype(F32) + total[:, kvd:] * gv[:, col(me)].astype(F32),
        axis=1, keepdims=True,
    )
    st_t[...] = to_rows(sq_t, inner)
    stats_send(0, st_t, sr_t)
    gather_finish(1, gk_block)
    gather_finish(2, gv_block)
    stats_end(0, st_t, sr_t, sc_t, co_t)
    kvt_out[...] = (kvt[...] * sc_t[:, 0:1]).astype(BF16)

    def text_copy(j):
        cs = pl.ds(pl.multiple_of(j * step, step), step)
        return pltpu.make_async_copy(tg.at[:, cs], tg_h.at[:, cs], tg_sem.at[j])

    def text_back(j, _):
        cs = pl.ds(pl.multiple_of(j * step, step), step)
        d = nt(gk[...], wk[cs, :]) + nt(gv[...], wv[cs, :])
        d = sc_t[:, 0:1] * (d * gain[:, cs]) - text[:, cs].astype(F32) * co_t[:, 0:1]
        tg[:, cs] = d.astype(BF16)
        text_copy(j).start()
        return 0

    lax.fori_loop(0, width // step, text_back, 0)

    total = level_end(1, i_own, i_l1, i_l2)
    kvi[...] = total
    inner = jnp.sum(
        total[:, :kvd] * gik[:, col(me)].astype(F32) + total[:, kvd:] * giv[:, col(me)].astype(F32),
        axis=1, keepdims=True,
    )
    st_i[...] = to_rows(sq_i, inner)
    stats_send(1, st_i, sr_i)
    gather_relay(3, gik_block)
    gather_relay(4, giv_block)
    gather_finish(3, gik_block)
    gather_finish(4, giv_block)

    def image_back(j, _):
        cs = pl.ds(pl.multiple_of(j * step, step), step)
        dg[:, cs] = (nt(gik[...], wk[cs, :]) + nt(giv[...], wv[cs, :])) * gain[:, cs]
        return 0

    lax.fori_loop(0, width // step, image_back, 0)
    stats_end(1, st_i, sr_i, sc_i, co_i)
    kvb[...] = (kvi[...] * sc_i[:, 0:1]).reshape(dp, rb, 2 * kvd).astype(BF16)
    r3[me_d] = kvb[me_d]

    def b1(k):
        return remote(kvb.at[dnext(k)], r3.at[me_d], b1_s.at[k], b1_r.at[k], (dnext(k), me))

    @pl.loop(1, dp)
    def _(k):
        b1(k).start()

    def image_end(j, _):
        cs = pl.ds(pl.multiple_of(j * step, step), step)
        d = sc_i[:, 0:1] * dg[:, cs] - emb[:, cs].astype(F32) * co_i[:, 0:1]
        dimg[:, cs] = d.astype(BF16)
        return 0

    lax.fori_loop(0, width // step, image_end, 0)

    pieces = d_send.shape[0]
    span = dv // pieces

    def vis_chunk(j):
        d = nt(dimg[...], wp[j * span:(j + 1) * span, :]).reshape(ycount, 2, rows, span)
        for yi in range(ycount):
            a, b = d[yi, 0], d[yi, 1]
            first = core == 0
            d_own[j, yi] = jnp.where(first, a, b)
            d_send[j, yi] = jnp.where(first, b, a).astype(BF16)
        send(d_send.at[j], d_l1.at[j], dv_s.at[0, j, 0], dv_r.at[0, j, 0], (me_d, partner))

    def vis_two(j):
        arrived(d_l1.at[j], dv_s.at[0, j, 0], dv_r.at[0, j, 0])
        for k in range(1, ycount):
            yk = ynext(k)
            d_s2[j, k] = (d_own[j, yk] + d_l1[j, yk].astype(F32)).astype(BF16)
            send(d_s2.at[j, k], d_l2.at[j, k], dv_s.at[1, j, k], dv_r.at[1, j, k], (me_d, yk * 2 + core))

    def b2(k):
        return remote(s4.at[dnext(k)], r4.at[:, me_d], b2_s.at[k], b2_r.at[k], (dnext(k), me))

    for j in range(pieces):
        vis_chunk(j)
        if j > 0:
            vis_two(j - 1)
        if j == min(2, pieces - 1):

            @pl.loop(1, dp)
            def _(k):
                block = r3.at[dprev(k)]
                remote(block, block, b1_s.at[k], b1_r.at[k], (me_d, partner)).wait_recv()

            @pl.loop(0, dp)
            def _(d):
                for s in range(slots):
                    s4[d, s] = r3[owner_ref[d * slots + s]]

            for s in range(slots):
                r4[s, me_d] = s4[me_d, s]

            @pl.loop(1, dp)
            def _(k):
                b2(k).start()

    vis_two(pieces - 1)
    hs = []
    for j in range(pieces):
        d = d_own[j, y] + d_l1[j, y].astype(F32)
        for k in range(1, ycount):
            arrived(d_l2.at[j, k], dv_s.at[1, j, k], dv_r.at[1, j, k])
            d = d + d_l2[j, k].astype(F32)
        hs.append(d.astype(BF16).astype(F32))
    vf = vis[...].astype(F32)
    vscale = lax.rsqrt(jnp.mean(vf * vf, axis=1, keepdims=True) + 1e-06)
    h = jnp.concatenate(hs, axis=1) * vgain[...]
    v_inner = jnp.mean(h * vf, axis=1, keepdims=True)
    vg_out[...] = (vscale * h - vf * vscale * vscale * vscale * v_inner).astype(BF16)

    @pl.loop(1, dp)
    def _(k):
        block = r4.at[:, dprev(k)]
        remote(block, block, b2_s.at[k], b2_r.at[k], (me_d, partner)).wait_recv()

    kvs_out[...] = r4[...]

    for copy in sends:
        copy.wait_send()

    @pl.loop(1, dp)
    def _(k):
        a1(k, 0).wait_send()
        a1(k, 1).wait_send()
        a2(k, 0).wait_send()
        a2(k, 1).wait_send()
        b1(k).wait_send()
        b2(k).wait_send()

    @pl.loop(0, width // step)
    def _(j):
        text_copy(j).wait()


def shards(vision, vision_gain, image_slot, text_embed, w_proj, llm_gain, w_key, w_value, key_grad, value_grad):
    dp = lax.axis_size("dp")
    mp = lax.axis_size("mp")
    here = lax.axis_index("dp")
    tokens, width = text_embed.shape
    slots = tokens // PATCH
    rows, dv = vision.shape
    kvd = key_grad.shape[1]
    kv = kvd * mp
    img = rows * mp
    rb = PATCH // dp
    ys = mp // 2
    pieces = 5 if dv % 640 == 0 else 1
    span = dv // pieces
    slot_ids = jnp.arange(dp * slots, dtype=jnp.int32)
    hot = slot_ids[:, None] == image_slot[None, :]
    owner = jnp.sum(jnp.where(hot, jnp.arange(dp, dtype=jnp.int32)[None, :], 0), axis=1).astype(jnp.int32)
    V = pltpu.VMEM
    any_spec = pl.BlockSpec(memory_space=pl.ANY)
    vmem = pl.BlockSpec(memory_space=pltpu.VMEM)
    smem = pl.BlockSpec(memory_space=pltpu.SMEM)
    scratch = [
        V((rows, dv), BF16), V((mp, rows, dv), BF16), V((tokens, width), BF16), V((dv, width), BF16),
        V((width, kv), BF16), V((width, kv), BF16), V((tokens, width), BF16),
        V((tokens, kv), BF16), V((tokens, kv), BF16), V((img, kv), BF16), V((img, kv), BF16),
        V((img, width), BF16), V((img, width), BF16), V((img, width), BF16), V((img, width), F32),
    ]
    for n in (tokens, img):
        scratch += [
            V((ys, n, 2 * kvd), BF16), V((ys, n, 2 * kvd), F32), V((ys, n, 2 * kvd), BF16),
            V((ys, n, 2 * kvd), BF16), V((ys, n, 2 * kvd), BF16),
        ]
    scratch += [
        V((pieces, ys, rows, span), BF16), V((pieces, ys, rows, span), F32), V((pieces, ys, rows, span), BF16),
        V((pieces, ys, rows, span), BF16), V((pieces, ys, rows, span), BF16),
        V((tokens, 2 * kvd), F32), V((img, 2 * kvd), F32),
        V((8, tokens), F32), V((mp, 8, tokens), F32), V((8, img), F32), V((mp, 8, img), F32),
        V((tokens, 128), F32), V((tokens, 128), F32), V((img, 128), F32), V((img, 128), F32),
        V((dp * slots, rb, kvd), BF16), V((dp * slots, rb, kvd), BF16),
        V((dp, rb, kvd), BF16), V((dp, rb, kvd), BF16), V((dp, rb, kvd), BF16), V((dp, rb, kvd), BF16),
        V((dp, rb, 2 * kvd), BF16), V((dp, rb, 2 * kvd), BF16),
        V((dp, slots, rb, 2 * kvd), BF16), V((slots, dp, rb, 2 * kvd), BF16),
        V((tokens, width), BF16),
        DMA((9,)), DMA((5, 2, ys)), DMA((5, 2, ys)), DMA((2, 2, ys)), DMA((2, 2, ys)),
        DMA((2, mp)), DMA((2, mp)), DMA((2, pieces, ys)), DMA((2, pieces, ys)),
        DMA((2, dp)), DMA((2, dp)), DMA((2, dp)), DMA((2, dp)),
        DMA((dp,)), DMA((dp,)), DMA((dp,)), DMA((dp,)), DMA((width // 256,)),
    ]
    kvt, kvs, tg, vgrad = pl.pallas_call(
        functools.partial(kernel, dp, mp),
        out_shape=(
            jax.ShapeDtypeStruct((tokens, 2 * kvd), BF16),
            jax.ShapeDtypeStruct((slots, dp, rb, 2 * kvd), BF16),
            jax.ShapeDtypeStruct((tokens, width), BF16),
            jax.ShapeDtypeStruct((rows, dv), BF16),
        ),
        in_specs=[smem, smem, any_spec, vmem, any_spec, any_spec, vmem] + [any_spec] * 6,
        out_specs=(vmem, vmem, any_spec, vmem),
        scratch_shapes=scratch,
        compiler_params=pltpu.CompilerParams(
            collective_id=0, has_side_effects=True, vmem_limit_bytes=67043328
        ),
    )(
        image_slot, owner, vision, vision_gain[None, :], text_embed, w_proj, llm_gain[None, :],
        w_key, w_value, key_grad, value_grad,
        key_grad.reshape(slots, dp, rb, kvd), value_grad.reshape(slots, dp, rb, kvd),
    )
    near = slot_ids.reshape(dp, slots)[here]
    filled = jnp.any(near[:, None] == image_slot[None, :], axis=1)
    filled = jnp.repeat(filled, PATCH)[:, None]
    kv_final = jnp.where(filled, kvs.reshape(tokens, 2 * kvd), kvt)
    text_grad = jnp.where(filled, jnp.zeros_like(tg), tg)
    return kv_final[:, :kvd], kv_final[:, kvd:], text_grad, vgrad


def solution(mesh):
    placed = (
        P(("dp", "mp"), None),
        P(),
        P(),
        P("dp", "mp"),
        P(None, "mp"),
        P("mp"),
        P("mp", None),
        P("mp", None),
        P("dp", "mp"),
        P("dp", "mp"),
    )
    return jax.shard_map(
        shards,
        mesh=mesh,
        in_specs=placed,
        out_specs=(P("dp", "mp"), P("dp", "mp"), P("dp", "mp"), P(("dp", "mp"), None)),
        check_vma=False,
    )
```

```python
import functools

import jax
import jax.numpy as jnp
from jax import lax
from jax.experimental import pallas as pl
from jax.experimental.pallas import tpu as pltpu
from jax.sharding import PartitionSpec as P

PATCH = 256
F32 = jnp.float32
BF16 = jnp.bfloat16
NT = (((1,), (1,)), ((), ()))
DMA = pltpu.SemaphoreType.DMA


def nt(a, b):
    return lax.dot_general(a, b, NT, preferred_element_type=F32)


def remote(src, dst, send_sem, recv_sem, device):
    return pltpu.make_async_remote_copy(
        src_ref=src, dst_ref=dst, send_sem=send_sem, recv_sem=recv_sem,
        device_id=device, device_id_type=pl.DeviceIdType.MESH,
    )


def to_rows(sq, inner):
    lane = lax.broadcasted_iota(jnp.int32, (sq.shape[0], 128), 1)
    wide = jnp.where(lane == 0, sq, jnp.where(lane == 1, inner, 0.0))
    return jnp.transpose(wide)[:8]


def to_columns(rows):
    wide = jnp.transpose(jnp.concatenate([rows] * 16, axis=0))
    return wide[:, 0:1], wide[:, 1:2]


def kernel(
    dp, mp, slot_ref, vision_h, vgain, text_h, wp_h, gain, wk_h, wv_h, kg_h, vg_h, kg4, vg4,
    k_out, v_out, tg_h, vg_out,
    vis, vis_all, text, wp, wk, wv, xt, gk, gv, gik, giv, emb, xi, dimg, dg,
    t_send, t_own, t_l1, t_s2, t_l2, i_send, i_own, i_l1, i_s2, i_l2,
    d_send, d_own, d_l1, d_s2, d_l2, kvt, kvi,
    st_t, sr_t, st_i, sr_i, sc_t, co_t, sc_i, co_i,
    r1k, r1v, s2k, s2v, r2k, r2v, kvb, r3, s4, r4, tg,
    load_sem, ag_s, ag_r, rs_s, rs_r, st_s, st_r, dv_s, dv_r,
    a1_s, a1_r, a2_s, a2_r, b1_s, b1_r, b2_s, b2_r, tg_sem,
):
    me_d = lax.axis_index("dp")
    me = lax.axis_index("mp")
    ycount = mp // 2
    core = lax.rem(me, 2)
    y = lax.div(me, 2)
    partner = y * 2 + (1 - core)
    tokens, width = text.shape
    slots = tokens // PATCH
    kvd = gk.shape[1] // mp
    rows = vis.shape[0]
    dv = vis.shape[1]
    d_model = width * mp
    rb = r1k.shape[1]

    def ynext(k):
        return lax.rem(y + k, ycount)

    def yprev(k):
        return lax.rem(y + ycount - k, ycount)

    def dnext(k):
        return lax.rem(me_d + k, dp)

    def dprev(k):
        return lax.rem(me_d + dp - k, dp)

    def col(m):
        return pl.ds(pl.multiple_of(m * kvd, kvd), kvd)

    def owner_of(slot):
        found = jnp.int32(0)
        for i in range(dp):
            found = jnp.where(slot_ref[i] == slot, jnp.int32(i), found)
        return found

    def filled(s):
        found = jnp.int32(0)
        for i in range(dp):
            found = jnp.where(slot_ref[i] == me_d * slots + s, jnp.int32(1), found)
        return found.astype(F32)

    sends = []

    def send(*args):
        copy = remote(*args)
        copy.start()
        sends.append(copy)

    loads = [
        (vision_h, vis), (kg_h, gk.at[:, col(me)]), (vg_h, gv.at[:, col(me)]),
        (text_h, text), (wk_h, wk), (wv_h, wv), (wp_h, wp),
        (kg4.at[:, me_d], r1k.at[pl.ds(me_d * slots, slots)]),
        (vg4.at[:, me_d], r1v.at[pl.ds(me_d * slots, slots)]),
    ]
    loads = [pltpu.make_async_copy(a, b, load_sem.at[n]) for n, (a, b) in enumerate(loads)]
    for copy in loads:
        copy.start()

    barrier = pltpu.get_barrier_semaphore()

    @pl.loop(1, dp)
    def _(k):
        pl.semaphore_signal(barrier, inc=1, device_id=(dnext(k), me), device_id_type=pl.DeviceIdType.MESH)

    for k in range(1, mp):
        pl.semaphore_signal(
            barrier, inc=1, device_id=(me_d, lax.rem(me + k, mp)), device_id_type=pl.DeviceIdType.MESH
        )

    loads[0].wait()
    vf = vis[...].astype(F32)
    vscale = lax.rsqrt(jnp.mean(vf * vf, axis=1, keepdims=True) + 1e-06)
    vis_all[me] = (vf * vscale * vgain[...]).astype(BF16)
    pl.semaphore_wait(barrier, dp - 1 + mp - 1)

    def gather_start(g, block):
        for k in range(1, ycount):
            send(block(me), block(me), ag_s.at[g, 0, k], ag_r.at[g, 0, k], (me_d, ynext(k) * 2 + core))
        send(block(me), block(me), ag_s.at[g, 0, 0], ag_r.at[g, 0, 0], (me_d, partner))

    def arrived(block, send_sem, recv_sem):
        remote(block, block, send_sem, recv_sem, (me_d, partner)).wait_recv()

    def gather_relay(g, block):
        for k in range(1, ycount):
            got = block(yprev(k) * 2 + core)
            arrived(got, ag_s.at[g, 0, k], ag_r.at[g, 0, k])
            send(got, got, ag_s.at[g, 1, k], ag_r.at[g, 1, k], (me_d, partner))

    def gather_finish(g, block):
        arrived(block(partner), ag_s.at[g, 0, 0], ag_r.at[g, 0, 0])
        for k in range(1, ycount):
            arrived(block(yprev(k) * 2 + 1 - core), ag_s.at[g, 1, k], ag_r.at[g, 1, k])

    vis_block = lambda m: vis_all.at[m]
    gk_block = lambda m: gk.at[:, col(m)]
    gv_block = lambda m: gv.at[:, col(m)]
    gik_block = lambda m: gik.at[:, col(m)]
    giv_block = lambda m: giv.at[:, col(m)]

    gather_start(0, vis_block)

    mine = pl.ds(me_d * slots, slots)

    def a1(k, which):
        src, dst = ((kg4, r1k), (vg4, r1v))[which]
        return remote(
            src.at[:, dnext(k)], dst.at[mine], a1_s.at[which, k], a1_r.at[which, k], (dnext(k), me)
        )

    @pl.loop(1, dp)
    def _(k):
        a1(k, 0).start()
        a1(k, 1).start()

    loads[1].wait()
    loads[2].wait()
    gather_start(1, gk_block)
    gather_start(2, gv_block)

    def stage(x, n, psend, own, l1):
        def chunk(m):
            k_part = jnp.dot(x[...], wk[:, col(m)], preferred_element_type=F32)
            v_part = jnp.dot(x[...], wv[:, col(m)], preferred_element_type=F32)
            return k_part, v_part

        for k in range(ycount):
            yk = ynext(k)
            k_part, v_part = chunk(yk * 2 + 1 - core)
            psend[yk, :, :kvd] = k_part.astype(BF16)
            psend[yk, :, kvd:] = v_part.astype(BF16)
            send(psend.at[yk], l1.at[yk], rs_s.at[n, 0, k], rs_r.at[n, 0, k], (me_d, partner))
        for k in range(ycount):
            yk = ynext(k)
            k_part, v_part = chunk(yk * 2 + core)
            own[yk, :, :kvd] = k_part
            own[yk, :, kvd:] = v_part

    def level_two(n, own, l1, s2, l2):
        for k in range(ycount - 1, 0, -1):
            yk = ynext(k)
            arrived(l1.at[yk], rs_s.at[n, 0, k], rs_r.at[n, 0, k])
            s2[k] = (own[yk] + l1[yk].astype(F32)).astype(BF16)

    def level_go(n, s2, l2):
        for k in range(ycount - 1, 0, -1):
            send(s2.at[k], l2.at[k], rs_s.at[n, 1, k], rs_r.at[n, 1, k], (me_d, ynext(k) * 2 + core))

    def level_end(n, own, l1, l2):
        arrived(l1.at[y], rs_s.at[n, 0, 0], rs_r.at[n, 0, 0])
        total = own[y] + l1[y].astype(F32)
        for k in range(1, ycount):
            arrived(l2.at[k], rs_s.at[n, 1, k], rs_r.at[n, 1, k])
            total = total + l2[k].astype(F32)
        return total

    def stats_send(n, st, sr):
        for k in range(1, mp):
            send(st, sr.at[k], st_s.at[n, k], st_r.at[n, k], (me_d, lax.rem(me + k, mp)))

    def stats_end(n, st, sr, sc, co, keep):
        total = st[...]
        for k in range(1, mp):
            arrived(sr.at[k], st_s.at[n, k], st_r.at[n, k])
            total = total + sr[k]
        sq, inner = to_columns(total)
        scale = lax.rsqrt(sq / d_model + 1e-05)
        sc[...] = jnp.broadcast_to(scale * keep, sc.shape)
        co[...] = jnp.broadcast_to(scale * scale * scale * (inner / d_model) * keep, co.shape)

    loads[3].wait()
    tf = text[...].astype(F32)
    sq_t = jnp.sum(tf * tf, axis=1, keepdims=True)
    xt[...] = (tf * gain[...]).astype(BF16)
    loads[4].wait()
    loads[5].wait()
    stage(xt, 0, t_send, t_own, t_l1)
    gather_relay(0, vis_block)
    level_two(0, t_own, t_l1, t_s2, t_l2)

    gather_finish(0, vis_block)
    loads[6].wait()
    step = 256
    dimg_rows = mp * rows


    def project(j, acc):
        cs = pl.ds(pl.multiple_of(j * step, step), step)
        e = jnp.concatenate([vis_all[m] for m in range(mp)], axis=0)
        e = jnp.dot(e, wp[:, cs], preferred_element_type=F32).astype(BF16)
        emb[:, cs] = e
        ef = e.astype(F32)
        xi[:, cs] = (ef * gain[:, cs]).astype(BF16)
        return acc + jnp.sum(ef * ef, axis=1, keepdims=True)

    half = width // step // 2
    sq_i = lax.fori_loop(0, half, project, jnp.zeros((dimg_rows, 1), F32))

    loads[7].wait()
    loads[8].wait()

    @pl.loop(1, dp)
    def _(k):
        for which, dst in ((0, r1k), (1, r1v)):
            block = dst.at[pl.ds(dprev(k) * slots, slots)]
            remote(block, block, a1_s.at[which, k], a1_r.at[which, k], (me_d, partner)).wait_recv()

    @pl.loop(0, dp)
    def _(i):
        s2k[i] = r1k[slot_ref[i]]
        s2v[i] = r1v[slot_ref[i]]

    r2k[me_d] = s2k[me_d]
    r2v[me_d] = s2v[me_d]

    def a2(k, which):
        src, dst = ((s2k, r2k), (s2v, r2v))[which]
        return remote(
            src.at[dnext(k)], dst.at[me_d], a2_s.at[which, k], a2_r.at[which, k], (dnext(k), me)
        )

    @pl.loop(1, dp)
    def _(k):
        a2(k, 0).start()
        a2(k, 1).start()

    sq_i = lax.fori_loop(half, width // step, project, sq_i)
    stage(xi, 1, i_send, i_own, i_l1)
    level_two(1, i_own, i_l1, i_s2, i_l2)
    level_go(1, i_s2, i_l2)

    @pl.loop(1, dp)
    def _(k):
        for which, dst in ((0, r2k), (1, r2v)):
            block = dst.at[dprev(k)]
            remote(block, block, a2_s.at[which, k], a2_r.at[which, k], (me_d, partner)).wait_recv()

    own_k = r2k[...].astype(F32).reshape(PATCH, kvd)
    own_v = r2v[...].astype(F32).reshape(PATCH, kvd)
    gik[:, col(me)] = own_k.astype(BF16)
    giv[:, col(me)] = own_v.astype(BF16)
    gather_start(3, gik_block)
    gather_start(4, giv_block)
    level_go(0, t_s2, t_l2)
    gather_relay(1, gk_block)
    gather_relay(2, gv_block)

    total = level_end(1, i_own, i_l1, i_l2)
    kvi[...] = total
    inner = jnp.sum(
        total[:, :kvd] * gik[:, col(me)].astype(F32) + total[:, kvd:] * giv[:, col(me)].astype(F32),
        axis=1, keepdims=True,
    )
    st_i[...] = to_rows(sq_i, inner)
    stats_send(1, st_i, sr_i)
    gather_relay(3, gik_block)
    gather_relay(4, giv_block)
    gather_finish(3, gik_block)
    gather_finish(4, giv_block)

    def image_back(j, _):
        cs = pl.ds(pl.multiple_of(j * step, step), step)
        dg[:, cs] = (nt(gik[...], wk[cs, :]) + nt(giv[...], wv[cs, :])) * gain[:, cs]
        return 0

    lax.fori_loop(0, width // step, image_back, 0)
    stats_end(1, st_i, sr_i, sc_i, co_i, 1.0)
    kvb[...] = (kvi[...] * sc_i[:, 0:1]).reshape(dp, rb, 2 * kvd).astype(BF16)
    r3[me_d] = kvb[me_d]

    def b1(k):
        return remote(kvb.at[dnext(k)], r3.at[me_d], b1_s.at[k], b1_r.at[k], (dnext(k), me))

    @pl.loop(1, dp)
    def _(k):
        b1(k).start()

    def image_end(j, _):
        cs = pl.ds(pl.multiple_of(j * step, step), step)
        d = sc_i[:, 0:1] * dg[:, cs] - emb[:, cs].astype(F32) * co_i[:, 0:1]
        dimg[:, cs] = d.astype(BF16)
        return 0

    lax.fori_loop(0, width // step, image_end, 0)

    pieces = d_send.shape[0]
    span = dv // pieces

    def vis_chunk(j):
        d = nt(dimg[...], wp[j * span:(j + 1) * span, :]).reshape(ycount, 2, rows, span)
        for yi in range(ycount):
            a, b = d[yi, 0], d[yi, 1]
            first = core == 0
            d_own[j, yi] = jnp.where(first, a, b)
            d_send[j, yi] = jnp.where(first, b, a).astype(BF16)
        send(d_send.at[j], d_l1.at[j], dv_s.at[0, j, 0], dv_r.at[0, j, 0], (me_d, partner))

    def vis_two(j):
        arrived(d_l1.at[j], dv_s.at[0, j, 0], dv_r.at[0, j, 0])
        for k in range(1, ycount):
            yk = ynext(k)
            d_s2[j, k] = (d_own[j, yk] + d_l1[j, yk].astype(F32)).astype(BF16)
            send(d_s2.at[j, k], d_l2.at[j, k], dv_s.at[1, j, k], dv_r.at[1, j, k], (me_d, yk * 2 + core))

    def b2(k):
        return remote(s4.at[dnext(k)], r4.at[:, me_d], b2_s.at[k], b2_r.at[k], (dnext(k), me))

    for j in range(pieces):
        vis_chunk(j)
        if j > 0:
            vis_two(j - 1)
        if j == min(2, pieces - 1):

            @pl.loop(1, dp)
            def _(k):
                block = r3.at[dprev(k)]
                remote(block, block, b1_s.at[k], b1_r.at[k], (me_d, partner)).wait_recv()

            @pl.loop(0, dp)
            def _(d):
                for s in range(slots):
                    s4[d, s] = r3[owner_of(d * slots + s)]

            for s in range(slots):
                r4[s, me_d] = s4[me_d, s]

            @pl.loop(1, dp)
            def _(k):
                b2(k).start()

    vis_two(pieces - 1)

    total = level_end(0, t_own, t_l1, t_l2)
    kvt[...] = total
    inner = jnp.sum(
        total[:, :kvd] * gk[:, col(me)].astype(F32) + total[:, kvd:] * gv[:, col(me)].astype(F32),
        axis=1, keepdims=True,
    )
    st_t[...] = to_rows(sq_t, inner)
    stats_send(0, st_t, sr_t)
    gather_finish(1, gk_block)
    gather_finish(2, gv_block)
    keep = jnp.concatenate([jnp.full((PATCH, 1), 1.0, F32) * (1.0 - filled(s)) for s in range(slots)], axis=0)
    stats_end(0, st_t, sr_t, sc_t, co_t, keep)

    def text_copy(j):
        cs = pl.ds(pl.multiple_of(j * step, step), step)
        return pltpu.make_async_copy(tg.at[:, cs], tg_h.at[:, cs], tg_sem.at[j])

    def text_back(j, _):
        cs = pl.ds(pl.multiple_of(j * step, step), step)
        d = nt(gk[...], wk[cs, :]) + nt(gv[...], wv[cs, :])
        d = sc_t[:, 0:1] * (d * gain[:, cs]) - text[:, cs].astype(F32) * co_t[:, 0:1]
        tg[:, cs] = d.astype(BF16)
        text_copy(j).start()
        return 0

    lax.fori_loop(0, width // step, text_back, 0)

    hs = []
    for j in range(pieces):
        d = d_own[j, y] + d_l1[j, y].astype(F32)
        for k in range(1, ycount):
            arrived(d_l2.at[j, k], dv_s.at[1, j, k], dv_r.at[1, j, k])
            d = d + d_l2[j, k].astype(F32)
        hs.append(d.astype(BF16).astype(F32))
    vf = vis[...].astype(F32)
    vscale = lax.rsqrt(jnp.mean(vf * vf, axis=1, keepdims=True) + 1e-06)
    h = jnp.concatenate(hs, axis=1) * vgain[...]
    v_inner = jnp.mean(h * vf, axis=1, keepdims=True)
    vg_out[...] = (vscale * h - vf * vscale * vscale * vscale * v_inner).astype(BF16)

    @pl.loop(1, dp)
    def _(k):
        block = r4.at[:, dprev(k)]
        remote(block, block, b2_s.at[k], b2_r.at[k], (me_d, partner)).wait_recv()

    for s in range(slots):
        at = pl.ds(s * PATCH, PATCH)
        out = kvt[at, :] * sc_t[at, 0:1] + r4[s].astype(F32).reshape(PATCH, 2 * kvd) * filled(s)
        k_out[at, :] = out[:, :kvd].astype(BF16)
        v_out[at, :] = out[:, kvd:].astype(BF16)

    for copy in sends:
        copy.wait_send()

    @pl.loop(1, dp)
    def _(k):
        a1(k, 0).wait_send()
        a1(k, 1).wait_send()
        a2(k, 0).wait_send()
        a2(k, 1).wait_send()
        b1(k).wait_send()
        b2(k).wait_send()

    @pl.loop(0, width // step)
    def _(j):
        text_copy(j).wait()


def shards(vision, vision_gain, image_slot, text_embed, w_proj, llm_gain, w_key, w_value, key_grad, value_grad):
    dp = lax.axis_size("dp")
    mp = lax.axis_size("mp")
    tokens, width = text_embed.shape
    slots = tokens // PATCH
    rows, dv = vision.shape
    kvd = key_grad.shape[1]
    kv = kvd * mp
    img = rows * mp
    rb = PATCH // dp
    ys = mp // 2
    pieces = 5 if dv % 640 == 0 else 1
    span = dv // pieces
    V = pltpu.VMEM
    any_spec = pl.BlockSpec(memory_space=pl.ANY)
    vmem = pl.BlockSpec(memory_space=pltpu.VMEM)
    smem = pl.BlockSpec(memory_space=pltpu.SMEM)
    scratch = [
        V((rows, dv), BF16), V((mp, rows, dv), BF16), V((tokens, width), BF16), V((dv, width), BF16),
        V((width, kv), BF16), V((width, kv), BF16), V((tokens, width), BF16),
        V((tokens, kv), BF16), V((tokens, kv), BF16), V((img, kv), BF16), V((img, kv), BF16),
        V((img, width), BF16), V((img, width), BF16), V((img, width), BF16), V((img, width), F32),
    ]
    for n in (tokens, img):
        scratch += [
            V((ys, n, 2 * kvd), BF16), V((ys, n, 2 * kvd), F32), V((ys, n, 2 * kvd), BF16),
            V((ys, n, 2 * kvd), BF16), V((ys, n, 2 * kvd), BF16),
        ]
    scratch += [
        V((pieces, ys, rows, span), BF16), V((pieces, ys, rows, span), F32), V((pieces, ys, rows, span), BF16),
        V((pieces, ys, rows, span), BF16), V((pieces, ys, rows, span), BF16),
        V((tokens, 2 * kvd), F32), V((img, 2 * kvd), F32),
        V((8, tokens), F32), V((mp, 8, tokens), F32), V((8, img), F32), V((mp, 8, img), F32),
        V((tokens, 128), F32), V((tokens, 128), F32), V((img, 128), F32), V((img, 128), F32),
        V((dp * slots, rb, kvd), BF16), V((dp * slots, rb, kvd), BF16),
        V((dp, rb, kvd), BF16), V((dp, rb, kvd), BF16), V((dp, rb, kvd), BF16), V((dp, rb, kvd), BF16),
        V((dp, rb, 2 * kvd), BF16), V((dp, rb, 2 * kvd), BF16),
        V((dp, slots, rb, 2 * kvd), BF16), V((slots, dp, rb, 2 * kvd), BF16),
        V((tokens, width), BF16),
        DMA((9,)), DMA((5, 2, ys)), DMA((5, 2, ys)), DMA((2, 2, ys)), DMA((2, 2, ys)),
        DMA((2, mp)), DMA((2, mp)), DMA((2, pieces, ys)), DMA((2, pieces, ys)),
        DMA((2, dp)), DMA((2, dp)), DMA((2, dp)), DMA((2, dp)),
        DMA((dp,)), DMA((dp,)), DMA((dp,)), DMA((dp,)), DMA((width // 256,)),
    ]
    return pl.pallas_call(
        functools.partial(kernel, dp, mp),
        out_shape=(
            jax.ShapeDtypeStruct((tokens, kvd), BF16),
            jax.ShapeDtypeStruct((tokens, kvd), BF16),
            jax.ShapeDtypeStruct((tokens, width), BF16),
            jax.ShapeDtypeStruct((rows, dv), BF16),
        ),
        in_specs=[smem, any_spec, vmem, any_spec, any_spec, vmem] + [any_spec] * 6,
        out_specs=(vmem, vmem, any_spec, vmem),
        scratch_shapes=scratch,
        compiler_params=pltpu.CompilerParams(
            collective_id=0, has_side_effects=True, vmem_limit_bytes=67043328
        ),
    )(
        image_slot, vision, vision_gain[None, :], text_embed, w_proj, llm_gain[None, :],
        w_key, w_value, key_grad, value_grad,
        key_grad.reshape(slots, dp, rb, kvd), value_grad.reshape(slots, dp, rb, kvd),
    )


def solution(mesh):
    placed = (
        P(("dp", "mp"), None),
        P(),
        P(),
        P("dp", "mp"),
        P(None, "mp"),
        P("mp"),
        P("mp", None),
        P("mp", None),
        P("dp", "mp"),
        P("dp", "mp"),
    )
    return jax.shard_map(
        shards,
        mesh=mesh,
        in_specs=placed,
        out_specs=(P("dp", "mp"), P("dp", "mp"), P("dp", "mp"), P(("dp", "mp"), None)),
        check_vma=False,
    )
```

```python
import functools

import jax
import jax.numpy as jnp
from jax import lax
from jax.experimental import pallas as pl
from jax.experimental.pallas import tpu as pltpu
from jax.sharding import PartitionSpec as P

PATCH = 256
F32 = jnp.float32
BF16 = jnp.bfloat16
NT = (((1,), (1,)), ((), ()))
DMA = pltpu.SemaphoreType.DMA


def nt(a, b):
    return lax.dot_general(a, b, NT, preferred_element_type=F32)


def remote(src, dst, send_sem, recv_sem, device):
    return pltpu.make_async_remote_copy(
        src_ref=src, dst_ref=dst, send_sem=send_sem, recv_sem=recv_sem,
        device_id=device, device_id_type=pl.DeviceIdType.MESH,
    )


def to_rows(sq, inner):
    lane = lax.broadcasted_iota(jnp.int32, (sq.shape[0], 128), 1)
    wide = jnp.where(lane == 0, sq, jnp.where(lane == 1, inner, 0.0))
    return jnp.transpose(wide)[:8]


def to_columns(rows):
    wide = jnp.transpose(jnp.concatenate([rows] * 16, axis=0))
    return wide[:, 0:1], wide[:, 1:2]


def kernel(
    dp, mp, slot_ref, vision_h, vgain, text_h, wp_h, gain, wk_h, wv_h, kg_h, vg_h, kg4, vg4,
    k_out, v_out, tg_h, vg_out,
    vis, vis_all, text, wp, wk, wv, xt, gk, gv, gik, giv, emb, xi, dimg, dg,
    t_send, t_own, t_l1, t_s2, t_l2, i_send, i_own, i_l1, i_s2, i_l2,
    d_send, d_own, d_l1, d_s2, d_l2, kvt, kvi,
    st_t, sr_t, st_i, sr_i, sc_t, co_t, sc_i, co_i,
    r1k, r1v, s2k, s2v, r2k, r2v, kvb, r3, s4, r4, tg,
    load_sem, ag_s, ag_r, rs_s, rs_r, st_s, st_r, dv_s, dv_r,
    a1_s, a1_r, a2_s, a2_r, b1_s, b1_r, b2_s, b2_r, tg_sem, dt,
):
    me_d = lax.axis_index("dp")
    me = lax.axis_index("mp")
    ycount = mp // 2
    core = lax.rem(me, 2)
    y = lax.div(me, 2)
    partner = y * 2 + (1 - core)
    tokens, width = text.shape
    slots = tokens // PATCH
    kvd = gk.shape[1] // mp
    rows = vis.shape[0]
    dv = vis.shape[1]
    d_model = width * mp
    rb = r1k.shape[1]

    def ynext(k):
        return lax.rem(y + k, ycount)

    def yprev(k):
        return lax.rem(y + ycount - k, ycount)

    def dnext(k):
        return lax.rem(me_d + k, dp)

    def dprev(k):
        return lax.rem(me_d + dp - k, dp)

    def col(m):
        return pl.ds(pl.multiple_of(m * kvd, kvd), kvd)

    def owner_of(slot):
        found = jnp.int32(0)
        for i in range(dp):
            found = jnp.where(slot_ref[i] == slot, jnp.int32(i), found)
        return found

    def filled(s):
        found = jnp.int32(0)
        for i in range(dp):
            found = jnp.where(slot_ref[i] == me_d * slots + s, jnp.int32(1), found)
        return found.astype(F32)

    sends = []

    def send(*args):
        copy = remote(*args)
        copy.start()
        sends.append(copy)

    loads = [
        (vision_h, vis), (kg_h, gk.at[:, col(me)]), (vg_h, gv.at[:, col(me)]),
        (text_h, text), (wk_h, wk), (wv_h, wv), (wp_h, wp),
        (kg4.at[:, me_d], r1k.at[pl.ds(me_d * slots, slots)]),
        (vg4.at[:, me_d], r1v.at[pl.ds(me_d * slots, slots)]),
    ]
    loads = [pltpu.make_async_copy(a, b, load_sem.at[n]) for n, (a, b) in enumerate(loads)]
    for copy in loads:
        copy.start()

    barrier = pltpu.get_barrier_semaphore()

    @pl.loop(1, dp)
    def _(k):
        pl.semaphore_signal(barrier, inc=1, device_id=(dnext(k), me), device_id_type=pl.DeviceIdType.MESH)

    for k in range(1, mp):
        pl.semaphore_signal(
            barrier, inc=1, device_id=(me_d, lax.rem(me + k, mp)), device_id_type=pl.DeviceIdType.MESH
        )

    loads[0].wait()
    vf = vis[...].astype(F32)
    vscale = lax.rsqrt(jnp.mean(vf * vf, axis=1, keepdims=True) + 1e-06)
    vis_all[me] = (vf * vscale * vgain[...]).astype(BF16)
    pl.semaphore_wait(barrier, dp - 1 + mp - 1)

    def gather_start(g, block):
        for k in range(1, ycount):
            send(block(me), block(me), ag_s.at[g, 0, k], ag_r.at[g, 0, k], (me_d, ynext(k) * 2 + core))
        send(block(me), block(me), ag_s.at[g, 0, 0], ag_r.at[g, 0, 0], (me_d, partner))

    def arrived(block, send_sem, recv_sem):
        remote(block, block, send_sem, recv_sem, (me_d, partner)).wait_recv()

    def gather_relay(g, block):
        for k in range(1, ycount):
            got = block(yprev(k) * 2 + core)
            arrived(got, ag_s.at[g, 0, k], ag_r.at[g, 0, k])
            send(got, got, ag_s.at[g, 1, k], ag_r.at[g, 1, k], (me_d, partner))

    def gather_finish(g, block):
        arrived(block(partner), ag_s.at[g, 0, 0], ag_r.at[g, 0, 0])
        for k in range(1, ycount):
            arrived(block(yprev(k) * 2 + 1 - core), ag_s.at[g, 1, k], ag_r.at[g, 1, k])

    vis_block = lambda m: vis_all.at[m]
    gk_block = lambda m: gk.at[:, col(m)]
    gv_block = lambda m: gv.at[:, col(m)]
    gik_block = lambda m: gik.at[:, col(m)]
    giv_block = lambda m: giv.at[:, col(m)]

    gather_start(0, vis_block)

    mine = pl.ds(me_d * slots, slots)

    def a1(k, which):
        src, dst = ((kg4, r1k), (vg4, r1v))[which]
        return remote(
            src.at[:, dnext(k)], dst.at[mine], a1_s.at[which, k], a1_r.at[which, k], (dnext(k), me)
        )

    @pl.loop(1, dp)
    def _(k):
        a1(k, 0).start()
        a1(k, 1).start()

    loads[1].wait()
    loads[2].wait()
    gather_start(1, gk_block)
    gather_start(2, gv_block)

    def stage(x, n, psend, own, l1):
        def chunk(m):
            k_part = jnp.dot(x[...], wk[:, col(m)], preferred_element_type=F32)
            v_part = jnp.dot(x[...], wv[:, col(m)], preferred_element_type=F32)
            return k_part, v_part

        for k in range(ycount):
            yk = ynext(k)
            k_part, v_part = chunk(yk * 2 + 1 - core)
            psend[yk, :, :kvd] = k_part.astype(BF16)
            psend[yk, :, kvd:] = v_part.astype(BF16)
            send(psend.at[yk], l1.at[yk], rs_s.at[n, 0, k], rs_r.at[n, 0, k], (me_d, partner))
        for k in range(ycount):
            yk = ynext(k)
            k_part, v_part = chunk(yk * 2 + core)
            own[yk, :, :kvd] = k_part
            own[yk, :, kvd:] = v_part

    def level_two(n, own, l1, s2, l2):
        for k in range(ycount - 1, 0, -1):
            yk = ynext(k)
            arrived(l1.at[yk], rs_s.at[n, 0, k], rs_r.at[n, 0, k])
            s2[k] = (own[yk] + l1[yk].astype(F32)).astype(BF16)

    def level_go(n, s2, l2):
        for k in range(ycount - 1, 0, -1):
            send(s2.at[k], l2.at[k], rs_s.at[n, 1, k], rs_r.at[n, 1, k], (me_d, ynext(k) * 2 + core))

    def level_end(n, own, l1, l2):
        arrived(l1.at[y], rs_s.at[n, 0, 0], rs_r.at[n, 0, 0])
        total = own[y] + l1[y].astype(F32)
        for k in range(1, ycount):
            arrived(l2.at[k], rs_s.at[n, 1, k], rs_r.at[n, 1, k])
            total = total + l2[k].astype(F32)
        return total

    def stats_send(n, st, sr):
        for k in range(1, mp):
            send(st, sr.at[k], st_s.at[n, k], st_r.at[n, k], (me_d, lax.rem(me + k, mp)))

    def stats_end(n, st, sr, sc, co, keep):
        total = st[...]
        for k in range(1, mp):
            arrived(sr.at[k], st_s.at[n, k], st_r.at[n, k])
            total = total + sr[k]
        sq, inner = to_columns(total)
        scale = lax.rsqrt(sq / d_model + 1e-05)
        sc[...] = jnp.broadcast_to(scale * keep, sc.shape)
        co[...] = jnp.broadcast_to(scale * scale * scale * (inner / d_model) * keep, co.shape)

    loads[3].wait()
    tf = text[...].astype(F32)
    sq_t = jnp.sum(tf * tf, axis=1, keepdims=True)
    xt[...] = (tf * gain[...]).astype(BF16)
    loads[4].wait()
    loads[5].wait()
    stage(xt, 0, t_send, t_own, t_l1)
    gather_relay(0, vis_block)
    level_two(0, t_own, t_l1, t_s2, t_l2)

    gather_finish(0, vis_block)
    loads[6].wait()
    step = 256
    dimg_rows = mp * rows


    def project(j, acc):
        cs = pl.ds(pl.multiple_of(j * step, step), step)
        e = jnp.concatenate([vis_all[m] for m in range(mp)], axis=0)
        e = jnp.dot(e, wp[:, cs], preferred_element_type=F32).astype(BF16)
        emb[:, cs] = e
        ef = e.astype(F32)
        xi[:, cs] = (ef * gain[:, cs]).astype(BF16)
        return acc + jnp.sum(ef * ef, axis=1, keepdims=True)

    half = width // step // 2
    sq_i = lax.fori_loop(0, half, project, jnp.zeros((dimg_rows, 1), F32))

    loads[7].wait()
    loads[8].wait()

    @pl.loop(1, dp)
    def _(k):
        for which, dst in ((0, r1k), (1, r1v)):
            block = dst.at[pl.ds(dprev(k) * slots, slots)]
            remote(block, block, a1_s.at[which, k], a1_r.at[which, k], (me_d, partner)).wait_recv()

    @pl.loop(0, dp)
    def _(i):
        s2k[i] = r1k[slot_ref[i]]
        s2v[i] = r1v[slot_ref[i]]

    r2k[me_d] = s2k[me_d]
    r2v[me_d] = s2v[me_d]

    def a2(k, which):
        src, dst = ((s2k, r2k), (s2v, r2v))[which]
        return remote(
            src.at[dnext(k)], dst.at[me_d], a2_s.at[which, k], a2_r.at[which, k], (dnext(k), me)
        )

    @pl.loop(1, dp)
    def _(k):
        a2(k, 0).start()
        a2(k, 1).start()

    sq_i = lax.fori_loop(half, width // step, project, sq_i)
    stage(xi, 1, i_send, i_own, i_l1)
    level_two(1, i_own, i_l1, i_s2, i_l2)
    level_go(1, i_s2, i_l2)

    @pl.loop(1, dp)
    def _(k):
        for which, dst in ((0, r2k), (1, r2v)):
            block = dst.at[dprev(k)]
            remote(block, block, a2_s.at[which, k], a2_r.at[which, k], (me_d, partner)).wait_recv()

    own_k = r2k[...].astype(F32).reshape(PATCH, kvd)
    own_v = r2v[...].astype(F32).reshape(PATCH, kvd)
    gik[:, col(me)] = own_k.astype(BF16)
    giv[:, col(me)] = own_v.astype(BF16)
    gather_start(3, gik_block)
    gather_start(4, giv_block)
    level_go(0, t_s2, t_l2)
    gather_relay(1, gk_block)
    gather_relay(2, gv_block)
    gather_finish(1, gk_block)
    gather_finish(2, gv_block)

    def text_product(j, _):
        cs = pl.ds(pl.multiple_of(j * step, step), step)
        dt[:, cs] = (nt(gk[...], wk[cs, :]) + nt(gv[...], wv[cs, :])) * gain[:, cs]
        return 0

    lax.fori_loop(0, width // step, text_product, 0)

    total = level_end(1, i_own, i_l1, i_l2)
    kvi[...] = total
    inner = jnp.sum(
        total[:, :kvd] * gik[:, col(me)].astype(F32) + total[:, kvd:] * giv[:, col(me)].astype(F32),
        axis=1, keepdims=True,
    )
    st_i[...] = to_rows(sq_i, inner)
    stats_send(1, st_i, sr_i)
    gather_relay(3, gik_block)
    gather_relay(4, giv_block)
    gather_finish(3, gik_block)
    gather_finish(4, giv_block)

    def image_back(j, _):
        cs = pl.ds(pl.multiple_of(j * step, step), step)
        dg[:, cs] = (nt(gik[...], wk[cs, :]) + nt(giv[...], wv[cs, :])) * gain[:, cs]
        return 0

    lax.fori_loop(0, width // step, image_back, 0)
    stats_end(1, st_i, sr_i, sc_i, co_i, 1.0)
    kvb[...] = (kvi[...] * sc_i[:, 0:1]).reshape(dp, rb, 2 * kvd).astype(BF16)
    r3[me_d] = kvb[me_d]

    def b1(k):
        return remote(kvb.at[dnext(k)], r3.at[me_d], b1_s.at[k], b1_r.at[k], (dnext(k), me))

    @pl.loop(1, dp)
    def _(k):
        b1(k).start()

    def image_end(j, _):
        cs = pl.ds(pl.multiple_of(j * step, step), step)
        d = sc_i[:, 0:1] * dg[:, cs] - emb[:, cs].astype(F32) * co_i[:, 0:1]
        dimg[:, cs] = d.astype(BF16)
        return 0

    lax.fori_loop(0, width // step, image_end, 0)

    pieces = d_send.shape[0]
    span = dv // pieces

    def vis_chunk(j):
        d = nt(dimg[...], wp[j * span:(j + 1) * span, :]).reshape(ycount, 2, rows, span)
        for yi in range(ycount):
            a, b = d[yi, 0], d[yi, 1]
            first = core == 0
            d_own[j, yi] = jnp.where(first, a, b)
            d_send[j, yi] = jnp.where(first, b, a).astype(BF16)
        send(d_send.at[j], d_l1.at[j], dv_s.at[0, j, 0], dv_r.at[0, j, 0], (me_d, partner))

    def vis_two(j):
        arrived(d_l1.at[j], dv_s.at[0, j, 0], dv_r.at[0, j, 0])
        for k in range(1, ycount):
            yk = ynext(k)
            d_s2[j, k] = (d_own[j, yk] + d_l1[j, yk].astype(F32)).astype(BF16)
            send(d_s2.at[j, k], d_l2.at[j, k], dv_s.at[1, j, k], dv_r.at[1, j, k], (me_d, yk * 2 + core))

    def b2(k):
        return remote(s4.at[dnext(k)], r4.at[:, me_d], b2_s.at[k], b2_r.at[k], (dnext(k), me))

    for j in range(pieces):
        vis_chunk(j)
        if j > 0:
            vis_two(j - 1)
        if j == min(2, pieces - 1):

            @pl.loop(1, dp)
            def _(k):
                block = r3.at[dprev(k)]
                remote(block, block, b1_s.at[k], b1_r.at[k], (me_d, partner)).wait_recv()

            @pl.loop(0, dp)
            def _(d):
                for s in range(slots):
                    s4[d, s] = r3[owner_of(d * slots + s)]

            for s in range(slots):
                r4[s, me_d] = s4[me_d, s]

            @pl.loop(1, dp)
            def _(k):
                b2(k).start()

    vis_two(pieces - 1)

    total = level_end(0, t_own, t_l1, t_l2)
    kvt[...] = total
    inner = jnp.sum(
        total[:, :kvd] * gk[:, col(me)].astype(F32) + total[:, kvd:] * gv[:, col(me)].astype(F32),
        axis=1, keepdims=True,
    )
    st_t[...] = to_rows(sq_t, inner)
    stats_send(0, st_t, sr_t)
    keep = jnp.concatenate([jnp.full((PATCH, 1), 1.0, F32) * (1.0 - filled(s)) for s in range(slots)], axis=0)
    stats_end(0, st_t, sr_t, sc_t, co_t, keep)

    def text_copy(j):
        cs = pl.ds(pl.multiple_of(j * step, step), step)
        return pltpu.make_async_copy(tg.at[:, cs], tg_h.at[:, cs], tg_sem.at[j])

    def text_back(j, _):
        cs = pl.ds(pl.multiple_of(j * step, step), step)
        d = sc_t[:, 0:1] * dt[:, cs] - text[:, cs].astype(F32) * co_t[:, 0:1]
        tg[:, cs] = d.astype(BF16)
        text_copy(j).start()
        return 0

    lax.fori_loop(0, width // step, text_back, 0)

    hs = []
    for j in range(pieces):
        d = d_own[j, y] + d_l1[j, y].astype(F32)
        for k in range(1, ycount):
            arrived(d_l2.at[j, k], dv_s.at[1, j, k], dv_r.at[1, j, k])
            d = d + d_l2[j, k].astype(F32)
        hs.append(d.astype(BF16).astype(F32))
    vf = vis[...].astype(F32)
    vscale = lax.rsqrt(jnp.mean(vf * vf, axis=1, keepdims=True) + 1e-06)
    h = jnp.concatenate(hs, axis=1) * vgain[...]
    v_inner = jnp.mean(h * vf, axis=1, keepdims=True)
    vg_out[...] = (vscale * h - vf * vscale * vscale * vscale * v_inner).astype(BF16)

    @pl.loop(1, dp)
    def _(k):
        block = r4.at[:, dprev(k)]
        remote(block, block, b2_s.at[k], b2_r.at[k], (me_d, partner)).wait_recv()

    for s in range(slots):
        at = pl.ds(s * PATCH, PATCH)
        out = kvt[at, :] * sc_t[at, 0:1] + r4[s].astype(F32).reshape(PATCH, 2 * kvd) * filled(s)
        k_out[at, :] = out[:, :kvd].astype(BF16)
        v_out[at, :] = out[:, kvd:].astype(BF16)

    for copy in sends:
        copy.wait_send()

    @pl.loop(1, dp)
    def _(k):
        a1(k, 0).wait_send()
        a1(k, 1).wait_send()
        a2(k, 0).wait_send()
        a2(k, 1).wait_send()
        b1(k).wait_send()
        b2(k).wait_send()

    @pl.loop(0, width // step)
    def _(j):
        text_copy(j).wait()


def shards(vision, vision_gain, image_slot, text_embed, w_proj, llm_gain, w_key, w_value, key_grad, value_grad):
    dp = lax.axis_size("dp")
    mp = lax.axis_size("mp")
    tokens, width = text_embed.shape
    slots = tokens // PATCH
    rows, dv = vision.shape
    kvd = key_grad.shape[1]
    kv = kvd * mp
    img = rows * mp
    rb = PATCH // dp
    ys = mp // 2
    pieces = 5 if dv % 640 == 0 else 1
    span = dv // pieces
    V = pltpu.VMEM
    any_spec = pl.BlockSpec(memory_space=pl.ANY)
    vmem = pl.BlockSpec(memory_space=pltpu.VMEM)
    smem = pl.BlockSpec(memory_space=pltpu.SMEM)
    scratch = [
        V((rows, dv), BF16), V((mp, rows, dv), BF16), V((tokens, width), BF16), V((dv, width), BF16),
        V((width, kv), BF16), V((width, kv), BF16), V((tokens, width), BF16),
        V((tokens, kv), BF16), V((tokens, kv), BF16), V((img, kv), BF16), V((img, kv), BF16),
        V((img, width), BF16), V((img, width), BF16), V((img, width), BF16), V((img, width), F32),
    ]
    for n in (tokens, img):
        scratch += [
            V((ys, n, 2 * kvd), BF16), V((ys, n, 2 * kvd), F32), V((ys, n, 2 * kvd), BF16),
            V((ys, n, 2 * kvd), BF16), V((ys, n, 2 * kvd), BF16),
        ]
    scratch += [
        V((pieces, ys, rows, span), BF16), V((pieces, ys, rows, span), F32), V((pieces, ys, rows, span), BF16),
        V((pieces, ys, rows, span), BF16), V((pieces, ys, rows, span), BF16),
        V((tokens, 2 * kvd), F32), V((img, 2 * kvd), F32),
        V((8, tokens), F32), V((mp, 8, tokens), F32), V((8, img), F32), V((mp, 8, img), F32),
        V((tokens, 128), F32), V((tokens, 128), F32), V((img, 128), F32), V((img, 128), F32),
        V((dp * slots, rb, kvd), BF16), V((dp * slots, rb, kvd), BF16),
        V((dp, rb, kvd), BF16), V((dp, rb, kvd), BF16), V((dp, rb, kvd), BF16), V((dp, rb, kvd), BF16),
        V((dp, rb, 2 * kvd), BF16), V((dp, rb, 2 * kvd), BF16),
        V((dp, slots, rb, 2 * kvd), BF16), V((slots, dp, rb, 2 * kvd), BF16),
        V((tokens, width), BF16),
        DMA((9,)), DMA((5, 2, ys)), DMA((5, 2, ys)), DMA((2, 2, ys)), DMA((2, 2, ys)),
        DMA((2, mp)), DMA((2, mp)), DMA((2, pieces, ys)), DMA((2, pieces, ys)),
        DMA((2, dp)), DMA((2, dp)), DMA((2, dp)), DMA((2, dp)),
        DMA((dp,)), DMA((dp,)), DMA((dp,)), DMA((dp,)), DMA((width // 256,)), V((tokens, width), F32),
    ]
    return pl.pallas_call(
        functools.partial(kernel, dp, mp),
        out_shape=(
            jax.ShapeDtypeStruct((tokens, kvd), BF16),
            jax.ShapeDtypeStruct((tokens, kvd), BF16),
            jax.ShapeDtypeStruct((tokens, width), BF16),
            jax.ShapeDtypeStruct((rows, dv), BF16),
        ),
        in_specs=[smem, any_spec, vmem, any_spec, any_spec, vmem] + [any_spec] * 6,
        out_specs=(vmem, vmem, any_spec, vmem),
        scratch_shapes=scratch,
        compiler_params=pltpu.CompilerParams(
            collective_id=0, has_side_effects=True, vmem_limit_bytes=67043328
        ),
    )(
        image_slot, vision, vision_gain[None, :], text_embed, w_proj, llm_gain[None, :],
        w_key, w_value, key_grad, value_grad,
        key_grad.reshape(slots, dp, rb, kvd), value_grad.reshape(slots, dp, rb, kvd),
    )


def solution(mesh):
    placed = (
        P(("dp", "mp"), None),
        P(),
        P(),
        P("dp", "mp"),
        P(None, "mp"),
        P("mp"),
        P("mp", None),
        P("mp", None),
        P("dp", "mp"),
        P("dp", "mp"),
    )
    return jax.shard_map(
        shards,
        mesh=mesh,
        in_specs=placed,
        out_specs=(P("dp", "mp"), P("dp", "mp"), P("dp", "mp"), P(("dp", "mp"), None)),
        check_vma=False,
    )
```
